32 devices in a mesh: ctx: 8 (over y, x, core), fsdp: 4 (over z).
Axes of the slice: x: 2, y: 2, z: 4, core: 2. Of those that a mesh axis runs over, the one named last changes fastest.
Arguments:
- inputs: bfloat16 [4, 1024, 2048], P('fsdp', 'ctx'), may hold values from -24 to 24
- block_order: int32 [16], replicated, may hold values from 0 to 15, each once
- norm_gains: bfloat16 [2, 2048], P(None, 'fsdp'), may hold values from 0.099609375 to 1.8984375
- w_query: bfloat16 [2048, 2048], P('fsdp'), may hold values from -0.125 to 0.125
- w_key: bfloat16 [256, 2048], P('fsdp'), may hold values from -0.125 to 0.125
- w_value: bfloat16 [256, 2048], P('fsdp'), may hold values from -0.125 to 0.125
- w_output: bfloat16 [2048, 2048], P('fsdp'), may hold values from -3 to 3
- w_gate: bfloat16 [5632, 2048], P('fsdp'), may hold values from -0.125 to 0.125
- w_up: bfloat16 [5632, 2048], P('fsdp'), may hold values from -0.125 to 0.125
- w_down: bfloat16 [2048, 5632], P('fsdp'), may hold values from -0.078125 to 0.078125
- out_grad: bfloat16 [4, 1024, 2048], P('fsdp', 'ctx'), may hold values from -6 to 6
Outputs:
- layer_out: bfloat16 [4, 1024, 2048], P('fsdp', 'ctx')
- grad_inputs: float32 [4, 1024, 2048], P('fsdp', 'ctx')
- grad_gains: float32 [2, 2048], P(None, 'fsdp')
- grad_query: float32 [2048, 2048], P('fsdp', 'ctx')
- grad_key: float32 [256, 2048], P('fsdp', 'ctx')
- grad_value: float32 [256, 2048], P('fsdp', 'ctx')
- grad_output: float32 [2048, 2048], P('fsdp', 'ctx')
- grad_gate: float32 [5632, 2048], P('fsdp', 'ctx')
- grad_up: float32 [5632, 2048], P('fsdp', 'ctx')
- grad_down: float32 [2048, 5632], P('fsdp', 'ctx')
The draws below stay inside these ranges and needn't reach their ends.
All inputs are finite; a program needn't handle non-finite values.
Results may differ from the reference program's by a relative error of at most 0.022.
Values may be sent and summed in bfloat16 or wider, within the bound.
No kernel may reach another device: no remote copies, remote signals or barrier semaphores. Data moves between devices by JAX's collectives and lax.ppermute only.
A program may use at most 320 MiB of HBM per device.

```python
import math
import jax
import jax.numpy as jnp
from jax import lax

D = 2048
FF = 5632
HEADS = 32
KV_HEADS = 4
HEAD_DIM = 64
BLOCK = 512
SEQLEN = 1024
SEQS = 4
HALF = 64
NBLK = 16
KVW = 256


def draw_inputs(key, part):
    noise_key, row_key, column_key = jax.random.split(key, 3)
    full_shape = (SEQS, SEQLEN, D)
    row_scales = jnp.exp(jax.random.uniform(row_key, (SEQS, SEQLEN, 1), minval=math.log(0.4), maxval=math.log(4.0)))
    column_scales = jnp.exp(jax.random.uniform(column_key, (D,), minval=math.log(0.3), maxval=math.log(3.0)))
    base_noise = jax.random.normal(noise_key, full_shape)
    return jnp.clip(base_noise * row_scales * column_scales, -24.0, 24.0).astype(jnp.bfloat16)


def with_spikes(values, own_key, source, target, blocks, factor):
    def block_of(position):
        return (jnp.arange(values.shape[position]) // (values.shape[position] // blocks)).reshape((-1,) + (1,) * (values.ndim - 1 - position))

    first = jax.random.permutation(own_key, blocks)[block_of(target)]
    other_side = (block_of(target) + blocks // 2) % blocks
    return jnp.where((block_of(source) == first) | (block_of(source) == other_side), factor * values, values)


def shard_levels(key, dims, cuts, smallest, largest):
    level = 1.0
    for position, parts in cuts:
        heights = jax.random.uniform(jax.random.fold_in(jax.random.fold_in(key, 6), position), (parts,), jnp.float32, smallest / len(cuts), largest / len(cuts))
        level = level * jnp.repeat(jnp.exp(heights), dims[position] // parts).reshape((-1,) + (1,) * (len(dims) - 1 - position))
    return level


def centred(own_key, extent, deviation, most, shards=(), kind=jnp.bfloat16):
    values = jax.random.normal(own_key, extent, jnp.float32) * deviation
    if len(shards) > 0:
        values = shard_levels(own_key, extent, shards, -0.22, 0.18) * values
    return jnp.clip(values, min=-most, max=most).astype(kind)


def noise_with(key, dims, scale, bound, shards, heavy, kind=jnp.bfloat16):
    entries = scale * jax.random.normal(key, dims, jnp.float32)
    if shards:
        entries = entries * shard_levels(key, dims, shards, -0.22, 0.18)
    return jnp.clip(with_spikes(entries, jax.random.fold_in(key, 3), *heavy), -bound, bound).astype(kind)


def setup_inputs(seed: int = 0) -> dict:
    seeds = jax.random.split(jax.random.key(seed), 12)
    return {
        "inputs": draw_inputs(jax.random.fold_in(seeds[11], 71), 0),
        "block_order": jax.random.permutation(seeds[1], NBLK).astype(jnp.int32),
        "norm_gains": jnp.clip(1.0 + 0.18 * jax.random.normal(seeds[2], (2, D), jnp.float32), 0.099609375, 1.8984375).astype(jnp.bfloat16),
        "w_query": centred(seeds[3], (D, D), D ** -0.5, 0.125, ((0, 4),)),
        "w_key": centred(seeds[4], (KVW, D), D ** -0.5, 0.125, ((0, 4),)),
        "w_value": centred(seeds[5], (KVW, D), D ** -0.5, 0.125, ((0, 4),)),
        "w_output": centred(seeds[6], (D, D), (max(D // 512, 1)) ** -0.5, 3.0, ((0, 4),)),
        "w_gate": centred(seeds[7], (FF, D), D ** -0.5, 0.125, ((0, 4),)),
        "w_up": centred(seeds[8], (FF, D), D ** -0.5, 0.125, ((0, 4),)),
        "w_down": centred(seeds[9], (D, FF), FF ** -0.5, 0.078125, ((0, 4),)),
        "out_grad": noise_with(seeds[10], (SEQS, SEQLEN, D), 1.0, 6.0, ((0, 4), (1, 8)), (1, 2, 8, 2.0)),
    }


@jax.custom_vjp
def low(v):
    return lax.optimization_barrier(v.astype(jnp.bfloat16)).astype(jnp.float32)

@jax.custom_vjp
def low_back(v):
    return v

def low_keep(v):
    return (low(v), None)

def low_pass(kept, grad):
    return (grad,)

def back_keep(v):
    return (v, None)

def back_low(kept, grad):
    return (low(grad),)
low.defvjp(low_keep, low_pass)
low_back.defvjp(back_keep, back_low)
HIGHEST = lax.Precision.HIGHEST
rms_eps = 1e-05
rope_base = 10000.0
masked_score = -1e+30

def project(values, weight):
    return jnp.dot(values, weight.T, precision=HIGHEST)

def rms_scale(values, gain_row):
    return values * lax.rsqrt(lax.optimization_barrier(jnp.mean(values * values, axis=-1, keepdims=True)) + rms_eps) * gain_row

def rotate(values, cosine, sine_table):
    half_dim = values.shape[-1] // 2
    turned = jnp.concatenate([-values[..., half_dim:], values[..., :half_dim]], axis=-1)
    return values * cosine + turned * sine_table

def attend(query_rot, key_rot, value_low):
    groups = HEADS // KV_HEADS
    blocks = query_rot.reshape(SEQLEN // BLOCK, BLOCK, KV_HEADS, groups, HEAD_DIM)
    starts = jnp.arange(SEQLEN // BLOCK, dtype=jnp.int32) * BLOCK
    key_positions = jnp.arange(SEQLEN, dtype=jnp.int32)
    score_scale = HEAD_DIM ** (-0.5)

    def one_block(block_item):
        block_queries, start_row = block_item
        raw_scores = low_back(jnp.einsum('qgha,kga->ghqk', block_queries, key_rot, precision=HIGHEST))
        query_positions = start_row + jnp.arange(BLOCK, dtype=jnp.int32)
        visible = key_positions[None, :] <= query_positions[:, None]
        scores = jnp.where(visible, raw_scores * score_scale, masked_score)
        row_peak = lax.optimization_barrier(jnp.max(scores, axis=-1, keepdims=True))
        exponent = jnp.exp(scores - row_peak)
        attention = low(exponent / lax.optimization_barrier(jnp.sum(exponent, axis=-1, keepdims=True)))
        return jnp.einsum('ghqk,kga->qgha', attention, value_low, precision=HIGHEST)
    mixed_blocks = lax.map(jax.checkpoint(one_block), (blocks, starts))
    return mixed_blocks.reshape(SEQLEN, HEADS * HEAD_DIM)

def layer(sequence, gain_rows, w_query, w_key, w_value, w_output, w_gate, w_up, w_down):
    positions = jnp.arange(SEQLEN, dtype=jnp.int32).astype(jnp.float32)
    frequency = rope_base ** (-jnp.arange(0, HEAD_DIM, 2).astype(jnp.float32) / HEAD_DIM)
    angles = positions[:, None] * frequency[None, :]
    cosine = jnp.concatenate([jnp.cos(angles), jnp.cos(angles)], axis=-1)[:, None, :]
    sine_table = jnp.concatenate([jnp.sin(angles), jnp.sin(angles)], axis=-1)[:, None, :]
    normed_one = low(rms_scale(sequence, gain_rows[0]))
    query_lin = low_back(project(normed_one, w_query)).reshape(SEQLEN, HEADS, HEAD_DIM)
    key_lin = low_back(project(normed_one, w_key)).reshape(SEQLEN, KV_HEADS, HEAD_DIM)
    value_low = low(low_back(project(normed_one, w_value))).reshape(SEQLEN, KV_HEADS, HEAD_DIM)
    query_rot = low(rotate(query_lin, cosine, sine_table))
    key_rot = low(rotate(key_lin, cosine, sine_table))
    mixed_low = low(low_back(attend(query_rot, key_rot, value_low)))
    hidden = sequence + low_back(project(mixed_low, w_output))
    normed_two = low(rms_scale(hidden, gain_rows[1]))
    gate_lin = low_back(project(normed_two, w_gate))
    up_lin = low_back(project(normed_two, w_up))
    inner_low = low(gate_lin * jax.nn.sigmoid(gate_lin) * up_lin)
    return hidden + low_back(project(inner_low, w_down))

def reorder(array, order):
    blocks = array.reshape(SEQS, NBLK, HALF, array.shape[-1])
    return jnp.take(blocks, order, axis=1).reshape(array.shape)

def reference(inputs, block_order, norm_gains, w_query, w_key, w_value, w_output, w_gate, w_up, w_down, out_grad):
    inverse_order = jnp.argsort(block_order).astype(jnp.int32)
    logical_in = reorder(inputs.astype(jnp.float32), inverse_order)
    logical_cot = reorder(out_grad.astype(jnp.float32), inverse_order)
    params = tuple((array.astype(jnp.float32) for array in (norm_gains, w_query, w_key, w_value, w_output, w_gate, w_up, w_down)))

    def one_sequence(totals, sample):
        sequence, cotangent = sample
        result, pullback = jax.vjp(layer, sequence, *params)
        gradient = pullback(cotangent)
        summed = tuple((running + addend for running, addend in zip(totals, gradient[1:])))
        return (summed, (result, gradient[0]))
    starting = tuple((jnp.zeros(array.shape, jnp.float32) for array in params))
    totals, (outputs, in_grads) = lax.scan(one_sequence, starting, (logical_in, logical_cot))
    layer_out = reorder(outputs, block_order).astype(jnp.bfloat16)
    grad_inputs = reorder(in_grads, block_order)
    return (layer_out, grad_inputs, totals[0], totals[1], totals[2], totals[3], totals[4], totals[5], totals[6], totals[7])
```

```python
import jax
import jax.numpy as jnp
from jax import lax
from jax.experimental import pallas as pl
from jax.experimental.pallas import tpu as pltpu
from jax.sharding import PartitionSpec as P

HEADS = 32
KV_HEADS = 4
HEAD_DIM = 64
HALF_DIM = HEAD_DIM // 2

rms_eps = 1e-05
rope_base = 10000.0
masked_score = -1e30
score_scale = HEAD_DIM ** (-0.5)

f32 = jnp.float32
bf16 = jnp.bfloat16


def dot(a, b, ca, cb):
    return lax.dot_general(a, b, (((ca,), (cb,)), ((), ())), preferred_element_type=f32)


def unpack_keys(kv_ref, kn, vn, kt, vt):
    blocks, _, tokens = kv_ref.shape
    for b in range(blocks):
        span = slice(b * tokens, (b + 1) * tokens)
        both = kv_ref[b]
        kt[:, span] = both[:HEAD_DIM]
        vt[:, span] = both[HEAD_DIM:]
        turned = both.T
        kn[span, :] = turned[:, :HEAD_DIM]
        vn[span, :] = turned[:, HEAD_DIM:]


def attend_forward_body(q_ref, kv_ref, bias_ref, o_ref, kn, vn, kt, vt):
    unpack_keys(kv_ref, kn, vn, kt, vt)
    heads = q_ref.shape[0] // HEAD_DIM
    bias = jnp.concatenate([bias_ref[...], bias_ref[...]], axis=1)
    tokens = q_ref.shape[1]
    for h in range(0, heads, 2):
        rows = [slice((h + i) * HEAD_DIM, (h + i + 1) * HEAD_DIM) for i in range(2)]
        q2 = jnp.concatenate([q_ref[r, :] for r in rows], axis=1)
        s = dot(kn[...], q2, 1, 0) + bias
        e = jnp.exp(s - jnp.max(s, axis=0, keepdims=True))
        inv = 1.0 / jnp.sum(e, axis=0, keepdims=True)
        o = dot(vt[...], (e * inv).astype(bf16), 1, 0)
        for i in range(2):
            o_ref[rows[i], :] = o[:, i * tokens : (i + 1) * tokens].astype(bf16)


def attend_backward_body(
    q_ref, kv_ref, bias_ref, do_ref, cos_ref, sin_ref, dq_ref, dkv_ref, kn, vn, kt, vt, dk, dv
):
    unpack_keys(kv_ref, kn, vn, kt, vt)
    heads = q_ref.shape[0] // HEAD_DIM
    bias = jnp.concatenate([bias_ref[...], bias_ref[...]], axis=1)
    tokens = q_ref.shape[1]
    cosine, sine = cos_ref[...], sin_ref[...]
    for h in range(0, heads, 2):
        rows = [slice((h + i) * HEAD_DIM, (h + i + 1) * HEAD_DIM) for i in range(2)]
        q2 = jnp.concatenate([q_ref[r, :] for r in rows], axis=1)
        do2 = jnp.concatenate([do_ref[r, :] for r in rows], axis=1)
        q_flat = jnp.concatenate([q_ref[r, :].T for r in rows], axis=0)
        do_flat = jnp.concatenate([do_ref[r, :].T for r in rows], axis=0)
        s = dot(kn[...], q2, 1, 0) + bias
        e = jnp.exp(s - jnp.max(s, axis=0, keepdims=True))
        p = e * (1.0 / jnp.sum(e, axis=0, keepdims=True))
        dp = dot(vn[...], do2, 1, 0)
        delta = jnp.sum(dp * p, axis=0, keepdims=True)
        ds = (p * (dp - delta)).astype(bf16)
        dv_part = dot(p.astype(bf16), do_flat, 1, 0)
        dk_part = dot(ds, q_flat, 1, 0)
        if h == 0:
            dk[...] = dk_part
            dv[...] = dv_part
        else:
            dk[...] += dk_part
            dv[...] += dv_part
        dq2 = dot(kt[...], ds, 1, 0) * score_scale
        for i in range(2):
            dq = dq2[:, i * tokens : (i + 1) * tokens]
            top, low = dq[:HALF_DIM], dq[HALF_DIM:]
            start = (h + i) * HEAD_DIM
            dq_ref[start : start + HALF_DIM, :] = (top * cosine + low * sine).astype(bf16)
            dq_ref[start + HALF_DIM : start + HEAD_DIM, :] = (low * cosine - top * sine).astype(bf16)
    blocks = kv_ref.shape[0]
    for b in range(blocks):
        span = slice(b * tokens, (b + 1) * tokens)
        dkv_ref[b, :HEAD_DIM, :] = dk[span, :].T.astype(bf16)
        dkv_ref[b, HEAD_DIM:, :] = dv[span, :].T.astype(bf16)


def key_scratch(keys):
    return [
        pltpu.VMEM((keys, HEAD_DIM), bf16),
        pltpu.VMEM((keys, HEAD_DIM), bf16),
        pltpu.VMEM((HEAD_DIM, keys), bf16),
        pltpu.VMEM((HEAD_DIM, keys), bf16),
    ]


def attend_forward(q, kv, bias):
    blocks, both, _ = kv.shape
    keys, tokens = bias.shape
    rows, columns = q.shape
    pieces = columns // tokens
    across = pl.BlockSpec((rows, tokens), lambda g: (0, g))
    elements = pieces * (rows // HEAD_DIM) * tokens * keys
    return pl.pallas_call(
        attend_forward_body,
        out_shape=jax.ShapeDtypeStruct(q.shape, bf16),
        grid=(pieces,),
        in_specs=[
            across,
            pl.BlockSpec((blocks, both, tokens), lambda g: (0, 0, g)),
            pl.BlockSpec((keys, tokens), lambda g: (0, 0)),
        ],
        out_specs=across,
        scratch_shapes=key_scratch(keys),
        cost_estimate=pl.CostEstimate(
            flops=4 * elements * HEAD_DIM,
            bytes_accessed=4 * q.size + 2 * kv.size,
            transcendentals=elements,
        ),
        name="attend_forward",
    )(q, kv, bias)


def attend_backward(q, kv, bias, d_out, cosine, sine):
    blocks, both, _ = kv.shape
    keys, tokens = bias.shape
    rows, columns = q.shape
    pieces = columns // tokens
    across = pl.BlockSpec((rows, tokens), lambda g: (0, g))
    whole = pl.BlockSpec((blocks, both, tokens), lambda g: (0, 0, g))
    table = pl.BlockSpec((HALF_DIM, tokens), lambda g: (0, 0))
    elements = pieces * (rows // HEAD_DIM) * tokens * keys
    return pl.pallas_call(
        attend_backward_body,
        out_shape=(jax.ShapeDtypeStruct(q.shape, bf16), jax.ShapeDtypeStruct(kv.shape, bf16)),
        grid=(pieces,),
        in_specs=[
            across,
            whole,
            pl.BlockSpec((keys, tokens), lambda g: (0, 0)),
            across,
            table,
            table,
        ],
        out_specs=(across, whole),
        scratch_shapes=key_scratch(keys)
        + [pltpu.VMEM((keys, HEAD_DIM), f32), pltpu.VMEM((keys, HEAD_DIM), f32)],
        cost_estimate=pl.CostEstimate(
            flops=10 * elements * HEAD_DIM,
            bytes_accessed=6 * q.size + 4 * kv.size,
            transcendentals=elements,
        ),
        name="attend_backward",
    )(q, kv, bias, d_out, cosine, sine)


def fetch(value, k, size):
    if k == 0:
        return value
    return lax.ppermute(value, "fsdp", [((i + k) % size, i) for i in range(size)])


def give(value, k, size):
    if k == 0:
        return value
    return lax.ppermute(value, "fsdp", [(i, (i + k) % size) for i in range(size)])


def spread_columns(weight, ctx_size, fsdp_size):
    rows, columns = weight.shape
    share, width = rows // ctx_size, columns // fsdp_size
    part = lax.dynamic_slice_in_dim(weight, lax.axis_index("ctx") * share, share)
    part = part.reshape(share, fsdp_size, width)
    part = lax.all_to_all(part, "fsdp", split_axis=1, concat_axis=0, tiled=True)
    part = part.reshape(fsdp_size, share, width)
    return lax.all_gather(part, "ctx", axis=1, tiled=True).reshape(rows * fsdp_size, width)


def return_columns(grad, ctx_size, fsdp_size):
    rows, width = grad.shape
    share = rows // (ctx_size * fsdp_size)
    part = grad.reshape(fsdp_size, ctx_size * share, width)
    part = lax.psum_scatter(part, "ctx", scatter_dimension=1, tiled=True)
    part = lax.all_to_all(part, "fsdp", split_axis=0, concat_axis=2, tiled=True)
    part = part.reshape(share, width * fsdp_size)
    return lax.all_to_all(part, "ctx", split_axis=1, concat_axis=0, tiled=True)


def joined(parts, axis=0):
    return parts[0] if len(parts) == 1 else jnp.concatenate(parts, axis=axis)


def inverse_norm(values):
    return lax.rsqrt(jnp.mean(values * values, axis=-1, keepdims=True) + rms_eps)


def per_device(
    inputs,
    block_order,
    norm_gains,
    w_query,
    w_key,
    w_value,
    w_output,
    w_gate,
    w_up,
    w_down,
    out_grad,
):
    C = lax.axis_size("ctx")
    F = lax.axis_size("fsdp")
    z = lax.axis_index("fsdp")
    c = lax.axis_index("ctx")
    tokens, width = inputs.shape[1:]
    keys = tokens * C
    own_x, own_dy = inputs[0], out_grad[0]
    sharing = max(1, F // KV_HEADS)
    kv_rows = w_key.shape[0]
    q_rows = w_query.shape[0]

    x_pieces = [fetch(own_x, k, F) for k in range(F)]
    gains = lax.all_gather(norm_gains, "fsdp", axis=1, tiled=True)
    dy_pieces = [fetch(own_dy, k, F) for k in range(F)]
    w_out = spread_columns(w_output, C, F)
    w_dn = spread_columns(w_down, C, F)

    half_len = keys // block_order.shape[0]
    offsets = jnp.arange(half_len, dtype=jnp.int32)
    key_pos = (block_order[:, None] * half_len + offsets[None, :]).reshape(keys)
    query_pos = lax.dynamic_slice_in_dim(key_pos, c * tokens, tokens)
    bias = jnp.where(key_pos[:, None] <= query_pos[None, :], 0.0, masked_score).astype(f32)
    frequency = rope_base ** (-jnp.arange(0, HEAD_DIM, 2).astype(f32) / HEAD_DIM)
    angles = frequency[:, None] * query_pos.astype(f32)[None, :]
    cosine, sine = jnp.cos(angles), jnp.sin(angles)
    gain_one, gain_two = gains[0].astype(f32), gains[1].astype(f32)

    if sharing > 1:
        groups = [[g * sharing + i for i in range(sharing)] for g in range(F // sharing)]
        both = jnp.stack([w_key, w_value])
        both = lax.all_gather(both, "fsdp", axis=1, tiled=True, axis_index_groups=groups)
        wk, wv = both[0], both[1]
    else:
        wk, wv = w_key, w_value
    w_qkv = jnp.concatenate([w_query, wk, wv], axis=0)

    x_all = joined(x_pieces).astype(f32)
    inv_all = inverse_norm(x_all)
    n1 = (x_all * inv_all * gain_one).astype(bf16)
    lin = dot(w_qkv, n1, 1, 1)

    def rope(values):
        v = values.reshape(-1, 2, HALF_DIM, F, tokens)
        cb, sb = cosine[:, None, :], sine[:, None, :]
        top, low = v[:, 0], v[:, 1]
        out = jnp.stack([top * cb - low * sb, low * cb + top * sb], axis=1)
        return out.reshape(values.shape)

    def rope_back(values):
        v = values.reshape(-1, 2, HALF_DIM, F, tokens)
        cb, sb = cosine[:, None, :], sine[:, None, :]
        top, low = v[:, 0], v[:, 1]
        out = jnp.stack([top * cb + low * sb, low * cb - top * sb], axis=1)
        return out.reshape(values.shape)

    q = (rope(lin[:q_rows]).astype(bf16)) * jnp.asarray(score_scale, bf16)
    kv_own = jnp.concatenate(
        [rope(lin[q_rows : q_rows + HEAD_DIM]).astype(bf16), lin[q_rows + HEAD_DIM :].astype(bf16)]
    )
    kv = lax.all_gather(kv_own, "ctx", axis=0)
    mixed = attend_forward(q, kv, bias)
    part = dot(mixed, w_out, 0, 1)
    hidden = own_x.astype(f32)
    for k in range(F):
        piece = part[k * tokens : (k + 1) * tokens]
        hidden = hidden + (piece if k == 0 else give(piece.astype(bf16), k, F).astype(f32))
    inv_two = inverse_norm(hidden)
    hat_two = hidden * inv_two
    own_n2 = (hat_two * gain_two).astype(bf16)

    n2 = joined([fetch(own_n2, k, F) for k in range(F)])
    dy = joined(dy_pieces)
    gate = dot(n2, w_gate, 1, 1)
    up = dot(n2, w_up, 1, 1)
    d_inner = dot(dy, w_dn, 1, 0)
    sig = jax.nn.sigmoid(gate)
    act = gate * sig
    inner = (act * up).astype(bf16)
    d_gate = (d_inner * up * sig * (1.0 + gate * (1.0 - sig))).astype(bf16)
    d_up = (d_inner * act).astype(bf16)
    dn2_part = dot(d_gate, w_gate, 1, 0) + dot(d_up, w_up, 1, 0)
    d_n2 = jnp.zeros((tokens, width), f32)
    for k in range(F):
        piece = dn2_part[k * tokens : (k + 1) * tokens]
        d_n2 = d_n2 + (piece if k == 0 else give(piece.astype(bf16), k, F).astype(f32))
    out_part = dot(inner, w_dn, 1, 1)
    layer = hidden
    for k in range(F):
        piece = out_part[k * tokens : (k + 1) * tokens]
        layer = layer + (piece if k == 0 else give(piece.astype(bf16), k, F).astype(f32))
    layer_out = layer.astype(bf16).reshape(1, tokens, width)

    scaled = d_n2 * gain_two
    inner_mean = jnp.mean(scaled * hidden, axis=-1, keepdims=True)
    d_hidden = own_dy.astype(f32) + inv_two * scaled - hidden * inv_two**3 * inner_mean
    gain_two_grad = jnp.sum(d_n2 * hat_two, axis=0)
    own_branch = d_hidden.astype(bf16)
    branch = joined([fetch(own_branch, k, F) for k in range(F)])

    d_mixed = dot(w_out, branch, 0, 1).astype(bf16)
    d_q, d_kv = attend_backward(q, kv, bias, d_mixed, cosine, sine)
    d_kv = lax.psum_scatter(d_kv, "ctx", scatter_dimension=0, tiled=False).astype(f32)
    if sharing > 1:
        d_kv = lax.psum(d_kv, "fsdp", axis_index_groups=groups)
    d_k = rope_back(d_kv[:HEAD_DIM]).astype(bf16)
    d_v = d_kv[HEAD_DIM:].astype(bf16)
    if sharing > 1:
        first = (z % sharing) * kv_rows
        d_k = lax.dynamic_slice_in_dim(d_k, first, kv_rows)
        d_v = lax.dynamic_slice_in_dim(d_v, first, kv_rows)
        w_own = jnp.concatenate([w_query, w_key, w_value], axis=0)
    else:
        w_own = w_qkv
    d_qkv = jnp.concatenate([d_q, d_k, d_v], axis=0)
    dn1_part = dot(d_qkv, w_own, 0, 0)
    d_n1 = jnp.zeros((tokens, width), f32)
    for k in range(F):
        piece = dn1_part[k * tokens : (k + 1) * tokens]
        d_n1 = d_n1 + (piece if k == 0 else give(piece.astype(bf16), k, F).astype(f32))
    rows = own_x.astype(f32)
    inv_one = inverse_norm(rows)
    scaled = d_n1 * gain_one
    inner_mean = jnp.mean(scaled * rows, axis=-1, keepdims=True)
    grad_inputs = d_hidden + inv_one * scaled - rows * inv_one**3 * inner_mean
    gain_one_grad = jnp.sum(d_n1 * rows * inv_one, axis=0)
    grad_inputs = grad_inputs.reshape(1, tokens, width)
    gain_totals = lax.psum(jnp.stack([gain_one_grad, gain_two_grad]), ("ctx", "fsdp"))
    gain_width = norm_gains.shape[1]
    grad_gains = lax.dynamic_slice_in_dim(gain_totals, z * gain_width, gain_width, 1)

    def reduced(value):
        return lax.psum_scatter(value.astype(bf16), "ctx", scatter_dimension=1, tiled=True).astype(f32)

    grad_gate = reduced(dot(d_gate, n2, 0, 0))
    grad_up = reduced(dot(d_up, n2, 0, 0))
    grad_down = return_columns(dot(dy, inner, 0, 0).astype(bf16), C, F).astype(f32)
    grad_out = return_columns(dot(branch, mixed, 0, 1).astype(bf16), C, F).astype(f32)
    g_qkv = reduced(dot(d_qkv, n1, 1, 0))
    grad_query = g_qkv[:q_rows]
    grad_key = g_qkv[q_rows : q_rows + kv_rows]
    grad_value = g_qkv[q_rows + kv_rows :]
    return (
        layer_out,
        grad_inputs,
        grad_gains,
        grad_query,
        grad_key,
        grad_value,
        grad_out,
        grad_gate,
        grad_up,
        grad_down,
    )


def solution(mesh):
    rows = P("fsdp", None)
    tokens = P("fsdp", "ctx", None)
    grads = P("fsdp", "ctx")
    return jax.shard_map(
        per_device,
        mesh=mesh,
        in_specs=(tokens, P(), P(None, "fsdp"), rows, rows, rows, rows, rows, rows, rows, tokens),
        out_specs=(tokens, tokens, P(None, "fsdp")) + (grads,) * 7,
        check_vma=False,
    )
```

```python
import jax
import jax.numpy as jnp
from jax import lax
from jax.experimental import pallas as pl
from jax.experimental.pallas import tpu as pltpu
from jax.sharding import PartitionSpec as P

KV_HEADS = 4
HEAD_DIM = 64
HALF_DIM = HEAD_DIM // 2

rms_eps = 1e-05
rope_base = 10000.0
masked_score = -1e30
score_scale = HEAD_DIM ** (-0.5)


f32 = jnp.float32
bf16 = jnp.bfloat16


def dot(a, b, ca, cb):
    return lax.dot_general(a, b, (((ca,), (cb,)), ((), ())), preferred_element_type=f32)


def unpack_keys(kv_ref, kn, vn, kt, vt):
    blocks, _, tokens = kv_ref.shape
    for b in range(blocks):
        span = slice(b * tokens, (b + 1) * tokens)
        both = kv_ref[b]
        kt[:, span] = both[:HEAD_DIM]
        vt[:, span] = both[HEAD_DIM:]
        turned = both.T
        kn[span, :] = turned[:, :HEAD_DIM]
        vn[span, :] = turned[:, HEAD_DIM:]


def attend_forward_body(q_ref, kv_ref, bias_ref, o_ref, kn, vn, kt, vt):
    unpack_keys(kv_ref, kn, vn, kt, vt)
    heads = q_ref.shape[0] // HEAD_DIM
    bias = jnp.concatenate([bias_ref[...], bias_ref[...]], axis=1)
    tokens = q_ref.shape[1]
    for h in range(0, heads, 2):
        rows = [slice((h + i) * HEAD_DIM, (h + i + 1) * HEAD_DIM) for i in range(2)]
        q2 = jnp.concatenate([q_ref[r, :] for r in rows], axis=1)
        s = dot(kn[...], q2, 1, 0) + bias
        e = jnp.exp(s - jnp.max(s, axis=0, keepdims=True))
        inv = 1.0 / jnp.sum(e, axis=0, keepdims=True)
        o = dot(vt[...], (e * inv).astype(bf16), 1, 0)
        for i in range(2):
            o_ref[rows[i], :] = o[:, i * tokens : (i + 1) * tokens].astype(bf16)


def attend_backward_body(
    q_ref, kv_ref, bias_ref, do_ref, cos_ref, sin_ref, dq_ref, dkv_ref, kn, vn, kt, vt, dk, dv
):
    unpack_keys(kv_ref, kn, vn, kt, vt)
    heads = q_ref.shape[0] // HEAD_DIM
    bias = jnp.concatenate([bias_ref[...], bias_ref[...]], axis=1)
    tokens = q_ref.shape[1]
    cosine, sine = cos_ref[...], sin_ref[...]
    for h in range(0, heads, 2):
        rows = [slice((h + i) * HEAD_DIM, (h + i + 1) * HEAD_DIM) for i in range(2)]
        q2 = jnp.concatenate([q_ref[r, :] for r in rows], axis=1)
        do2 = jnp.concatenate([do_ref[r, :] for r in rows], axis=1)
        q_flat = jnp.concatenate([q_ref[r, :].T for r in rows], axis=0)
        do_flat = jnp.concatenate([do_ref[r, :].T for r in rows], axis=0)
        s = dot(kn[...], q2, 1, 0) + bias
        e = jnp.exp(s - jnp.max(s, axis=0, keepdims=True))
        p = e * (1.0 / jnp.sum(e, axis=0, keepdims=True))
        dp = dot(vn[...], do2, 1, 0)
        delta = jnp.sum(dp * p, axis=0, keepdims=True)
        ds = (p * (dp - delta)).astype(bf16)
        dv_part = dot(p.astype(bf16), do_flat, 1, 0)
        dk_part = dot(ds, q_flat, 1, 0)
        if h == 0:
            dk[...] = dk_part
            dv[...] = dv_part
        else:
            dk[...] += dk_part
            dv[...] += dv_part
        dq2 = dot(kt[...], ds, 1, 0) * score_scale
        for i in range(2):
            dq = dq2[:, i * tokens : (i + 1) * tokens]
            top, low = dq[:HALF_DIM], dq[HALF_DIM:]
            start = (h + i) * HEAD_DIM
            dq_ref[start : start + HALF_DIM, :] = (top * cosine + low * sine).astype(bf16)
            dq_ref[start + HALF_DIM : start + HEAD_DIM, :] = (low * cosine - top * sine).astype(bf16)
    blocks = kv_ref.shape[0]
    for b in range(blocks):
        span = slice(b * tokens, (b + 1) * tokens)
        dkv_ref[b, :HEAD_DIM, :] = dk[span, :].T.astype(bf16)
        dkv_ref[b, HEAD_DIM:, :] = dv[span, :].T.astype(bf16)


def key_scratch(keys):
    return [
        pltpu.VMEM((keys, HEAD_DIM), bf16),
        pltpu.VMEM((keys, HEAD_DIM), bf16),
        pltpu.VMEM((HEAD_DIM, keys), bf16),
        pltpu.VMEM((HEAD_DIM, keys), bf16),
    ]


def attend_forward(q, kv, bias):
    blocks, both, _ = kv.shape
    keys, tokens = bias.shape
    rows, columns = q.shape
    pieces = columns // tokens
    across = pl.BlockSpec((rows, tokens), lambda g: (0, g))
    elements = pieces * (rows // HEAD_DIM) * tokens * keys
    return pl.pallas_call(
        attend_forward_body,
        out_shape=jax.ShapeDtypeStruct(q.shape, bf16),
        grid=(pieces,),
        in_specs=[
            across,
            pl.BlockSpec((blocks, both, tokens), lambda g: (0, 0, g)),
            pl.BlockSpec((keys, tokens), lambda g: (0, 0)),
        ],
        out_specs=across,
        scratch_shapes=key_scratch(keys),
        cost_estimate=pl.CostEstimate(
            flops=4 * elements * HEAD_DIM,
            bytes_accessed=4 * q.size + 2 * kv.size,
            transcendentals=elements,
        ),
        name="attend_forward",
    )(q, kv, bias)


def attend_backward(q, kv, bias, d_out, cosine, sine, first, earlier):
    blocks, both, _ = kv.shape
    keys, tokens = bias.shape
    rows = q.shape[0]
    pieces = d_out.shape[1] // tokens
    across = pl.BlockSpec((rows, tokens), lambda g: (0, g + first if first else g))
    whole = pl.BlockSpec((blocks, both, tokens), lambda g: (0, 0, g + first if first else g))
    table = pl.BlockSpec((HALF_DIM, tokens), lambda g: (0, 0))
    in_specs = [
        across,
        whole,
        pl.BlockSpec((keys, tokens), lambda g: (0, 0)),
        pl.BlockSpec((rows, tokens), lambda g: (0, g)),
        table,
        table,
    ]
    operands = [q, kv, bias, d_out, cosine, sine]
    aliases, body = {}, attend_backward_body
    if earlier is not None:
        in_specs += [pl.BlockSpec(memory_space=pl.ANY)] * 2
        aliases = {6: 0, 7: 1}
        operands += list(earlier)

        def body(*refs):
            attend_backward_body(*refs[:6], *refs[8:])

    elements = pieces * (rows // HEAD_DIM) * tokens * keys
    return pl.pallas_call(
        body,
        out_shape=(jax.ShapeDtypeStruct(q.shape, bf16), jax.ShapeDtypeStruct(kv.shape, bf16)),
        grid=(pieces,),
        in_specs=in_specs,
        out_specs=(across, whole),
        scratch_shapes=key_scratch(keys)
        + [pltpu.VMEM((keys, HEAD_DIM), f32), pltpu.VMEM((keys, HEAD_DIM), f32)],
        input_output_aliases=aliases,
        cost_estimate=pl.CostEstimate(
            flops=10 * elements * HEAD_DIM,
            bytes_accessed=(6 * q.size + 4 * kv.size) * tokens * pieces // q.shape[1],
            transcendentals=elements,
        ),
    )(*operands)


def fetch(value, k, size):
    return lax.ppermute(value, "fsdp", [((i + k) % size, i) for i in range(size)])


def give(value, k, size):
    return lax.ppermute(value, "fsdp", [(i, (i + k) % size) for i in range(size)])


def gather_pieces(value, size):
    if size != 4:
        return [value] + [fetch(value, k, size) for k in range(1, size)]
    after_one = fetch(value, 1, 4)
    before_one = fetch(value, 3, 4)
    down = lax.ppermute(after_one, "fsdp", [(1, 0), (2, 1)])
    up = lax.ppermute(before_one, "fsdp", [(1, 2), (2, 3)])
    return [value, after_one, jnp.where(lax.axis_index("fsdp") < 2, down, up), before_one]


def scatter_sum(parts, size):
    total = parts[0].astype(f32)
    if size != 4:
        for k in range(1, size):
            total = total + give(parts[k].astype(bf16), k, size).astype(f32)
        return total
    far = parts[2].astype(bf16)
    up = lax.ppermute(far, "fsdp", [(0, 1), (1, 2)])
    down = lax.ppermute(far, "fsdp", [(3, 2), (2, 1)])
    one = (parts[1].astype(f32) + up.astype(f32)).astype(bf16)
    after_one = give(one, 1, 4)
    one = (parts[3].astype(f32) + down.astype(f32)).astype(bf16)
    before_one = give(one, 3, 4)
    return total + after_one.astype(f32) + before_one.astype(f32)


def swap(value, mask):
    size = lax.axis_size("ctx")
    return lax.ppermute(value, "ctx", [(i, i ^ mask) for i in range(size)])


def masks_of(size, first):
    bits = [1 << i for i in range(1, size.bit_length() - 1)]
    return [1] + bits[::-1] if first else bits + [1]


def block_order_of(size):
    found = [0]
    for mask in masks_of(size, False):
        found = found + [m ^ mask for m in found]
    return found


def ctx_gather(value):
    value = value[None]
    for mask in masks_of(lax.axis_size("ctx"), False):
        value = jnp.concatenate([value, swap(value, mask)], axis=0)
    return value


def ctx_sum_back(value):
    for mask in masks_of(lax.axis_size("ctx"), True):
        half = value.shape[0] // 2
        come = swap(value[half:], mask)
        value = (value[:half].astype(f32) + come.astype(f32)).astype(value.dtype)
    return value[0]


def ctx_sum_exchange(value):
    come = lax.all_to_all(value, "ctx", split_axis=0, concat_axis=0, tiled=True)
    return jnp.sum(come.astype(f32), axis=0).astype(value.dtype)


def ctx_sum_scatter(value):
    size = lax.axis_size("ctx")
    c = lax.axis_index("ctx")

    def halve(v, axis, mask):
        bit = (c // mask) % 2
        kept = lax.dynamic_index_in_dim(v, bit, axis, False)
        sent = lax.dynamic_index_in_dim(v, 1 - bit, axis, False)
        come = swap(sent, mask)
        return (kept.astype(f32) + come.astype(f32)).astype(v.dtype)

    bits = size.bit_length() - 1
    v = value.reshape((2,) * bits + value.shape[1:])
    v = halve(v, bits - 1, 1)
    if bits != 3 or value.shape[1] % 32:
        for axis in range(bits - 2, -1, -1):
            v = halve(v, axis, 1 << (bits - 1 - axis))
        return v
    rows = value.shape[1] // 2
    one, two = halve(v[:, :, :rows], 1, 2), halve(v[:, :, rows:], 0, 4)
    return jnp.concatenate([halve(one, 0, 4), halve(two, 0, 2)], axis=0)


def column_blocks(weight, ctx_size, fsdp_size):
    rows, columns = weight.shape
    share, width = rows // ctx_size, columns // fsdp_size
    part = lax.dynamic_slice_in_dim(weight, lax.axis_index("ctx") * share, share)
    return part.reshape(share, fsdp_size, width).transpose(1, 0, 2)


def swap_blocks(blocks):
    return lax.all_to_all(blocks, "fsdp", split_axis=0, concat_axis=0, tiled=True)


def gather_rows(blocks):
    width = blocks.shape[2]
    return lax.all_gather(blocks, "ctx", axis=0).transpose(1, 0, 2, 3).reshape(-1, width)


def own_rows_of(parts, extra):
    F, share = parts[0].shape[:2]
    C = lax.axis_size("ctx")
    cuts = C // F
    widths = [p.shape[2] // cuts for p in parts]
    total = sum(widths)
    n = extra.shape[1]

    def rows_of(values, columns):
        lead, count = values.shape
        rows = -(-count // columns)
        values = jnp.pad(values, ((0, 0), (0, rows * columns - count)))
        return values.reshape(lead, rows, columns).astype(bf16)

    lines = rows_of(extra, total * cuts)
    come = swap_blocks(jnp.concatenate([jnp.concatenate(parts, axis=2), lines], axis=1))
    summed = jnp.sum(come[:, share:].astype(f32), axis=0).reshape(1, -1)[:, :n]
    pieces, start = [], 0
    for w in widths:
        piece = come[:, :share, start : start + w * cuts].reshape(F, share, cuts, w)
        pieces.append(piece.transpose(0, 2, 1, 3).reshape(C, share, w))
        start += w * cuts
    lines = jnp.broadcast_to(rows_of(summed, total), (C, -(-n // total), total))
    come = lax.all_to_all(
        jnp.concatenate([jnp.concatenate(pieces, axis=2), lines], axis=1),
        "ctx",
        split_axis=0,
        concat_axis=0,
        tiled=True,
    )
    summed = jnp.sum(come[:, share:].astype(f32), axis=0).reshape(-1)[:n]
    results, start = [], 0
    for w in widths:
        results.append(come[:, :share, start : start + w].reshape(C * share, w))
        start += w
    return results, summed


def row_shares(grad, ctx_size, fsdp_size):
    rows, width = grad.shape
    share = rows // (ctx_size * fsdp_size)
    grad = grad.reshape(fsdp_size, ctx_size, share, width).transpose(1, 0, 2, 3)
    return grad.reshape(rows, width)


def joined(parts, axis=0):
    return parts[0] if len(parts) == 1 else jnp.concatenate(parts, axis=axis)


def after(value, *others):
    return lax.optimization_barrier((value,) + others)[0]


def inverse_norm(values):
    return lax.rsqrt(jnp.mean(values * values, axis=-1, keepdims=True) + rms_eps)


def per_device(
    inputs,
    block_order,
    norm_gains,
    w_query,
    w_key,
    w_value,
    w_output,
    w_gate,
    w_up,
    w_down,
    out_grad,
):
    C = lax.axis_size("ctx")
    F = lax.axis_size("fsdp")
    z = lax.axis_index("fsdp")
    c = lax.axis_index("ctx")
    tokens, width = inputs.shape[1:]
    keys = tokens * C
    own_x, own_dy = inputs[0], out_grad[0]
    sharing = max(1, F // KV_HEADS)
    kv_rows = w_key.shape[0]
    q_rows = w_query.shape[0]
    gain_width = norm_gains.shape[1]
    order = [0, 1, 3, 2] if F == 4 else list(range(F))
    attention_groups = [order]
    backward_groups = [order[:3], order[3:]] if F == 4 else [order]
    ffn_groups = [order]

    x_pieces = gather_pieces(own_x, F)
    w_out_blocks = column_blocks(after(w_output, x_pieces[1]), C, F)
    share, _ = w_out_blocks.shape[1:]
    gain_blocks = jnp.broadcast_to(norm_gains[None], (F, 2, gain_width))
    swapped = swap_blocks(jnp.concatenate([w_out_blocks, gain_blocks], axis=1))
    w_out_rows = swapped[:, :share]
    gains = swapped[:, share:].transpose(1, 0, 2).reshape(2, F * gain_width)

    half_len = keys // block_order.shape[0]
    offsets = jnp.arange(half_len, dtype=jnp.int32)
    key_pos = (block_order[:, None] * half_len + offsets[None, :]).reshape(keys)
    query_pos = lax.dynamic_slice_in_dim(key_pos, c * tokens, tokens)
    members = jnp.asarray(block_order_of(C), jnp.int32) ^ c
    key_pos = jnp.take(key_pos.reshape(C, tokens), members, axis=0).reshape(keys)
    bias = jnp.where(key_pos[:, None] <= query_pos[None, :], 0.0, masked_score).astype(f32)
    frequency = rope_base ** (-jnp.arange(0, HEAD_DIM, 2).astype(f32) / HEAD_DIM)
    angles = frequency[:, None] * query_pos.astype(f32)[None, :]
    cosine, sine = jnp.cos(angles), jnp.sin(angles)
    gain_one, gain_two = gains[0].astype(f32), gains[1].astype(f32)

    if sharing > 1:
        sharers = [[g * sharing + i for i in range(sharing)] for g in range(F // sharing)]
        both = jnp.stack([w_key, w_value])
        both = lax.all_gather(both, "fsdp", axis=1, tiled=True, axis_index_groups=sharers)
        wk, wv = both[0], both[1]
    else:
        wk, wv = w_key, w_value
    w_qkv = jnp.concatenate([w_query, wk, wv], axis=0)

    def rope(values, sign):
        v = values.reshape(-1, 2, HALF_DIM, values.shape[1] // tokens, tokens)
        cb, sb = cosine[:, None, :], sign * sine[:, None, :]
        top, low = v[:, 0], v[:, 1]
        out = jnp.stack([top * cb - low * sb, low * cb + top * sb], axis=1)
        return out.reshape(values.shape)

    x_float = own_x.astype(f32)
    n1, q, kv, mixed, x_groups, inverses = [], [], [], [], [], []
    attn_parts = [None] * F
    for g, group in enumerate(attention_groups):
        x_group = joined([x_pieces[k] for k in group])
        if g == 0:
            x_group, w_out_rows = lax.optimization_barrier((x_group, w_out_rows))
            w_out = gather_rows(w_out_rows)
        inv_group = inverse_norm(x_group.astype(f32))
        n1_group = (x_group.astype(f32) * inv_group * gain_one).astype(bf16)
        x_groups.append(x_group)
        inverses.append(inv_group)
        lin = dot(w_qkv, n1_group, 1, 1)
        q_group = rope(lin[:q_rows], 1.0).astype(bf16) * jnp.asarray(score_scale, bf16)
        kv_own = jnp.concatenate(
            [
                rope(lin[q_rows : q_rows + HEAD_DIM], 1.0).astype(bf16),
                lin[q_rows + HEAD_DIM :].astype(bf16),
            ]
        )
        kv_group = ctx_gather(kv_own)
        if g == 0:
            down_blocks = swap_blocks(column_blocks(after(w_down, kv_own), C, F))
        mixed_group = attend_forward(q_group, kv_group, bias)
        part = dot(mixed_group, w_out, 0, 1)
        for i, k in enumerate(group):
            attn_parts[k] = part[i * tokens : (i + 1) * tokens]
        n1.append(n1_group)
        q.append(q_group)
        kv.append(kv_group)
        mixed.append(mixed_group)
    dy_late = after(own_dy, x_pieces[F // 2])
    dy_pieces = [dy_late]
    for k in range(1, F):
        dy_pieces.append(fetch(dy_late, k, F))
    w_dn = gather_rows(after(down_blocks, mixed[0]))
    hidden = x_float + scatter_sum(attn_parts, F)
    inv_two = inverse_norm(hidden)
    hat_two = hidden * inv_two
    own_n2 = (hat_two * gain_two).astype(bf16)

    n2_pieces = gather_pieces(own_n2, F)
    n2, dy, inner, d_gate, d_up = [], [], [], [], []
    dn2_parts = [None] * F
    out_parts = [None] * F
    for group in ffn_groups:
        n2_group = joined([n2_pieces[k] for k in group])
        dy_group = joined([dy_pieces[k] for k in group])
        gate = dot(n2_group, w_gate, 1, 1)
        up = dot(n2_group, w_up, 1, 1)
        d_inner = dot(dy_group, w_dn, 1, 0)
        sig = jax.nn.sigmoid(gate)
        act = gate * sig
        inner_group = (act * up).astype(bf16)
        d_gate_group = (d_inner * up * sig * (1.0 + gate * (1.0 - sig))).astype(bf16)
        d_up_group = (d_inner * act).astype(bf16)
        part = dot(d_gate_group, w_gate, 1, 0) + dot(d_up_group, w_up, 1, 0)
        out_part = dot(inner_group, w_dn, 1, 1)
        for i, k in enumerate(group):
            dn2_parts[k] = part[i * tokens : (i + 1) * tokens]
            out_parts[k] = out_part[i * tokens : (i + 1) * tokens].astype(bf16)
        n2.append(n2_group)
        dy.append(dy_group)
        inner.append(inner_group)
        d_gate.append(d_gate_group)
        d_up.append(d_up_group)
    n2, dy, inner, d_gate, d_up = (joined(v) for v in (n2, dy, inner, d_gate, d_up))
    d_n2 = scatter_sum(dn2_parts, F)

    part_down = row_shares(dot(dy, inner, 0, 0).astype(bf16), C, F)
    part_gate = dot(d_gate, n2, 0, 0).astype(bf16)
    part_up = dot(d_up, n2, 0, 0).astype(bf16)
    d_n2 = after(d_n2, part_down, part_gate, part_up)

    def reduced(value):
        return lax.psum_scatter(value, "ctx", scatter_dimension=1, tiled=True)

    part_down = lax.psum_scatter(part_down, "ctx", scatter_dimension=0, tiled=True)
    grad_gate = reduced(part_gate)
    grad_up = reduced(part_up)

    scaled = d_n2 * gain_two
    inner_mean = jnp.mean(scaled * hidden, axis=-1, keepdims=True)
    d_hidden = own_dy.astype(f32) + inv_two * scaled - hidden * inv_two**3 * inner_mean
    gain_two_grad = jnp.sum(d_n2 * hat_two, axis=0)
    branch_pieces = gather_pieces(d_hidden.astype(bf16), F)

    branch, grads, first = [], None, 0
    for group in backward_groups:
        branch_group = joined([branch_pieces[k] for k in group])
        d_mixed = dot(w_out, branch_group, 0, 1).astype(bf16)
        grads = attend_backward(q[0], kv[0], bias, d_mixed, cosine, sine, first, grads)
        first += len(group)
        branch.append(branch_group)
    d_q, d_kv = [grads[0]], [ctx_sum_back(grads[1])]
    d_qkv = []
    dn1_parts = [None] * F
    gain_one_grad = jnp.zeros((width,), f32)
    for g, group in enumerate(attention_groups):
        dkv_group = d_kv[g].astype(f32)
        if sharing > 1:
            dkv_group = lax.psum(dkv_group, "fsdp", axis_index_groups=sharers)
        d_k = rope(dkv_group[:HEAD_DIM], -1.0).astype(bf16)
        d_v = dkv_group[HEAD_DIM:].astype(bf16)
        if sharing > 1:
            first = (z % sharing) * kv_rows
            d_k = lax.dynamic_slice_in_dim(d_k, first, kv_rows)
            d_v = lax.dynamic_slice_in_dim(d_v, first, kv_rows)
            w_own = jnp.concatenate([w_query, w_key, w_value], axis=0)
        else:
            w_own = w_qkv
        d_qkv.append(jnp.concatenate([d_q[g], d_k, d_v], axis=0))
        part = dot(d_qkv[g], w_own, 0, 0).astype(bf16)
        hat = x_groups[g].astype(f32) * inverses[g]
        gain_one_grad = gain_one_grad + jnp.sum(part.astype(f32) * hat, axis=0)
        for i, k in enumerate(group):
            dn1_parts[k] = part[i * tokens : (i + 1) * tokens]
    d_n1 = scatter_sum(dn1_parts, F)

    layer = hidden + scatter_sum([after(p, branch_pieces[2]) for p in out_parts], F)
    layer_out = layer.astype(bf16).reshape(1, tokens, width)

    branch, mixed, n1, d_qkv = joined(branch), joined(mixed, 1), joined(n1), joined(d_qkv, 1)
    part_out = row_shares(dot(branch, mixed, 0, 1).astype(bf16), C, F)
    part_out = ctx_sum_exchange(part_out.reshape(C, width // C, -1))
    gain_parts = jnp.stack([gain_one_grad, gain_two_grad]).reshape(2, F, gain_width)
    gain_parts = gain_parts.transpose(1, 0, 2).reshape(F, 2 * gain_width)
    share = width // C // F
    (grad_down, grad_out), grad_gains = own_rows_of(
        [part_down.reshape(F, share, -1), part_out.reshape(F, share, -1)], gain_parts
    )
    grad_gains = grad_gains.reshape(2, gain_width)
    grad_down, grad_out = grad_down.astype(f32), grad_out.astype(f32)
    g_qkv = dot(n1, d_qkv, 0, 1).astype(bf16)
    g_qkv = ctx_sum_scatter(g_qkv.reshape(C, width // C, -1)).T.astype(f32)
    d_n1 = after(d_n1, grad_gains, grad_out, grad_down)
    grad_gate = after(grad_gate, d_n1).astype(f32)
    grad_up = after(grad_up, d_n1).astype(f32)

    inv_one = inverse_norm(x_float)
    scaled = d_n1 * gain_one
    inner_mean = jnp.mean(scaled * x_float, axis=-1, keepdims=True)
    grad_inputs = d_hidden + inv_one * scaled - x_float * inv_one**3 * inner_mean
    grad_inputs = grad_inputs.reshape(1, tokens, width)
    grad_query = g_qkv[:q_rows]
    grad_key = g_qkv[q_rows : q_rows + kv_rows]
    grad_value = g_qkv[q_rows + kv_rows :]
    return (
        layer_out,
        grad_inputs,
        grad_gains,
        grad_query,
        grad_key,
        grad_value,
        grad_out,
        grad_gate,
        grad_up,
        grad_down,
    )


def solution(mesh):
    rows = P("fsdp", None)
    tokens = P("fsdp", "ctx", None)
    grads = P("fsdp", "ctx")
    return jax.shard_map(
        per_device,
        mesh=mesh,
        in_specs=(tokens, P(), P(None, "fsdp"), rows, rows, rows, rows, rows, rows, rows, tokens),
        out_specs=(tokens, tokens, P(None, "fsdp")) + (grads,) * 7,
        check_vma=False,
    )
```

```python
import functools

import jax
import jax.numpy as jnp
from jax import lax
from jax.experimental import pallas as pl
from jax.experimental.pallas import tpu as pltpu
from jax.sharding import PartitionSpec as P

KV_HEADS = 4
HEAD_DIM = 64
HALF_DIM = HEAD_DIM // 2

rms_eps = 1e-05
rope_base = 10000.0
masked_score = -1e30
score_scale = HEAD_DIM ** (-0.5)


f32 = jnp.float32
bf16 = jnp.bfloat16


def dot(a, b, ca, cb):
    return lax.dot_general(a, b, (((ca,), (cb,)), ((), ())), preferred_element_type=f32)


def unpack_keys(kv_ref, kn, vn, kt, vt):
    blocks, _, tokens = kv_ref.shape
    for b in range(blocks):
        span = slice(b * tokens, (b + 1) * tokens)
        both = kv_ref[b]
        kt[:, span] = both[:HEAD_DIM]
        vt[:, span] = both[HEAD_DIM:]
        turned = both.T
        kn[span, :] = turned[:, :HEAD_DIM]
        vn[span, :] = turned[:, HEAD_DIM:]


def attend_forward_body(q_ref, kv_ref, bias_ref, o_ref, kn, vn, kt, vt):
    unpack_keys(kv_ref, kn, vn, kt, vt)
    heads = q_ref.shape[0] // HEAD_DIM
    bias = jnp.concatenate([bias_ref[...], bias_ref[...]], axis=1)
    tokens = q_ref.shape[1]
    for h in range(0, heads, 2):
        rows = [slice((h + i) * HEAD_DIM, (h + i + 1) * HEAD_DIM) for i in range(2)]
        q2 = jnp.concatenate([q_ref[r, :] for r in rows], axis=1)
        s = dot(kn[...], q2, 1, 0) + bias
        e = jnp.exp(s - jnp.max(s, axis=0, keepdims=True))
        inv = 1.0 / jnp.sum(e, axis=0, keepdims=True)
        o = dot(vt[...], e.astype(bf16), 1, 0) * inv
        for i in range(2):
            o_ref[rows[i], :] = o[:, i * tokens : (i + 1) * tokens].astype(bf16)


def attend_backward_body(
    q_ref, kv_ref, bias_ref, do_ref, cos_ref, sin_ref, dq_ref, dkv_ref, kn, vn, kt, vt, dk, dv
):
    unpack_keys(kv_ref, kn, vn, kt, vt)
    heads = q_ref.shape[0] // HEAD_DIM
    bias = jnp.concatenate([bias_ref[...], bias_ref[...]], axis=1)
    tokens = q_ref.shape[1]
    cosine, sine = cos_ref[...], sin_ref[...]
    for h in range(0, heads, 2):
        rows = [slice((h + i) * HEAD_DIM, (h + i + 1) * HEAD_DIM) for i in range(2)]
        q2 = jnp.concatenate([q_ref[r, :] for r in rows], axis=1)
        do2 = jnp.concatenate([do_ref[r, :] for r in rows], axis=1)
        q_flat = jnp.concatenate([q_ref[r, :].T for r in rows], axis=0)
        do_flat = jnp.concatenate([do_ref[r, :].T for r in rows], axis=0)
        s = dot(kn[...], q2, 1, 0) + bias
        e = jnp.exp(s - jnp.max(s, axis=0, keepdims=True))
        p = e * (1.0 / jnp.sum(e, axis=0, keepdims=True))
        dp = dot(vn[...], do2, 1, 0)
        delta = jnp.sum(dp * p, axis=0, keepdims=True)
        ds = (p * (dp - delta)).astype(bf16)
        dv_part = dot(p.astype(bf16), do_flat, 1, 0)
        dk_part = dot(ds, q_flat, 1, 0)
        if h == 0:
            dk[...] = dk_part
            dv[...] = dv_part
        else:
            dk[...] += dk_part
            dv[...] += dv_part
        dq2 = dot(kt[...], ds, 1, 0) * score_scale
        for i in range(2):
            dq = dq2[:, i * tokens : (i + 1) * tokens]
            top, low = dq[:HALF_DIM], dq[HALF_DIM:]
            start = (h + i) * HEAD_DIM
            dq_ref[start : start + HALF_DIM, :] = (top * cosine + low * sine).astype(bf16)
            dq_ref[start + HALF_DIM : start + HEAD_DIM, :] = (low * cosine - top * sine).astype(bf16)
    blocks = kv_ref.shape[0]
    for b in range(blocks):
        span = slice(b * tokens, (b + 1) * tokens)
        dkv_ref[b, :HEAD_DIM, :] = dk[span, :].T.astype(bf16)
        dkv_ref[b, HEAD_DIM:, :] = dv[span, :].T.astype(bf16)


def key_scratch(keys):
    return [
        pltpu.VMEM((keys, HEAD_DIM), bf16),
        pltpu.VMEM((keys, HEAD_DIM), bf16),
        pltpu.VMEM((HEAD_DIM, keys), bf16),
        pltpu.VMEM((HEAD_DIM, keys), bf16),
    ]


def attend_forward(q, kv, bias):
    blocks, both, _ = kv.shape
    keys, tokens = bias.shape
    rows, columns = q.shape
    pieces = columns // tokens
    across = pl.BlockSpec((rows, tokens), lambda g: (0, g))
    elements = pieces * (rows // HEAD_DIM) * tokens * keys
    return pl.pallas_call(
        attend_forward_body,
        out_shape=jax.ShapeDtypeStruct(q.shape, bf16),
        grid=(pieces,),
        in_specs=[
            across,
            pl.BlockSpec((blocks, both, tokens), lambda g: (0, 0, g)),
            pl.BlockSpec((keys, tokens), lambda g: (0, 0)),
        ],
        out_specs=across,
        scratch_shapes=key_scratch(keys),
        cost_estimate=pl.CostEstimate(
            flops=4 * elements * HEAD_DIM,
            bytes_accessed=4 * q.size + 2 * kv.size,
            transcendentals=elements,
        ),
        compiler_params=pltpu.CompilerParams(vmem_limit_bytes=20 * keys << 10),
        name="fwd",
    )(q, kv, bias)


def attend_backward(q, kv, bias, d_out, cosine, sine, first, earlier):
    blocks, both, _ = kv.shape
    keys, tokens = bias.shape
    rows = q.shape[0]
    pieces = d_out.shape[1] // tokens
    across = pl.BlockSpec((rows, tokens), lambda g: (0, g + first if first else g))
    whole = pl.BlockSpec((blocks, both, tokens), lambda g: (0, 0, g + first if first else g))
    table = pl.BlockSpec((HALF_DIM, tokens), lambda g: (0, 0))
    in_specs = [
        across,
        whole,
        pl.BlockSpec((keys, tokens), lambda g: (0, 0)),
        pl.BlockSpec((rows, tokens), lambda g: (0, g)),
        table,
        table,
    ]
    operands = [q, kv, bias, d_out, cosine, sine]
    aliases, body = {}, attend_backward_body
    if earlier is not None:
        in_specs += [pl.BlockSpec(memory_space=pl.ANY)] * 2
        aliases = {6: 0, 7: 1}
        operands += list(earlier)

        def body(*refs):
            attend_backward_body(*refs[:6], *refs[8:])

    elements = pieces * (rows // HEAD_DIM) * tokens * keys
    return pl.pallas_call(
        body,
        out_shape=(jax.ShapeDtypeStruct(q.shape, bf16), jax.ShapeDtypeStruct(kv.shape, bf16)),
        grid=(pieces,),
        in_specs=in_specs,
        out_specs=(across, whole),
        scratch_shapes=key_scratch(keys)
        + [pltpu.VMEM((keys, HEAD_DIM), f32), pltpu.VMEM((keys, HEAD_DIM), f32)],
        input_output_aliases=aliases,
        cost_estimate=pl.CostEstimate(
            flops=10 * elements * HEAD_DIM,
            bytes_accessed=(6 * q.size + 4 * kv.size) * tokens * pieces // q.shape[1],
            transcendentals=elements,
        ),
        compiler_params=pltpu.CompilerParams(vmem_limit_bytes=24 * keys << 10),
    )(*operands)


def feed_forward_body(count, carried, *refs):
    n2_refs, refs = refs[:count], refs[count:]
    dy_ref, wg_ref, wu_ref, wd_ref = refs[:4]
    refs = refs[4 + carried :]
    dn2_refs, out_refs, refs = refs[:count], refs[count : 2 * count], refs[2 * count :]
    inner_ref, both_ref, n2, acc_dn2, acc_out = refs
    tokens = n2_refs[0].shape[0]
    tile = wg_ref.shape[0]
    step = pl.program_id(0)

    @pl.when(step == 0)
    def _():
        for i, ref in enumerate(n2_refs):
            n2[i * tokens : (i + 1) * tokens, :] = ref[...]
        acc_dn2[...] = jnp.zeros_like(acc_dn2)
        acc_out[...] = jnp.zeros_like(acc_out)

    both = jnp.concatenate([wg_ref[...], wu_ref[...]], axis=0)
    gate_up = dot(n2[...], both, 1, 1)
    d_inner = dot(dy_ref[...], wd_ref[...], 1, 0)
    gate, up = gate_up[:, :tile], gate_up[:, tile:]
    sig = jax.nn.sigmoid(gate)
    act = gate * sig
    inner = (act * up).astype(bf16)
    d_gate = (d_inner * up * sig * (1.0 + gate * (1.0 - sig))).astype(bf16)
    d_up = (d_inner * act).astype(bf16)
    d_both = jnp.concatenate([d_gate, d_up], axis=1)
    inner_ref[...] = inner
    both_ref[...] = d_both
    acc_dn2[...] += dot(d_both, both, 1, 0)
    acc_out[...] += dot(inner, wd_ref[...], 1, 1)

    @pl.when(step == pl.num_programs(0) - 1)
    def _():
        for i in range(count):
            rows = slice(i * tokens, (i + 1) * tokens)
            dn2_refs[i][...] = acc_dn2[rows, :].astype(bf16)
            out_refs[i][...] = acc_out[rows, :].astype(bf16)


def feed_forward(n2_pieces, dy, w_gate, w_up, w_dn, first, earlier):
    count = len(n2_pieces)
    tokens, width = n2_pieces[0].shape
    rows = count * tokens
    hidden = w_gate.shape[0]
    tile = 128 if hidden % 128 == 0 else hidden
    block = first // count
    assert block * count == first
    piece = pl.BlockSpec((tokens, width), lambda j: (0, 0))
    strip = pl.BlockSpec((tile, width), lambda j: (j, 0))
    in_specs = [piece] * count + [
        pl.BlockSpec((rows, width), lambda j: (block, 0)),
        strip,
        strip,
        pl.BlockSpec((width, tile), lambda j: (0, j)),
    ]
    operands = [*n2_pieces, dy, w_gate, w_up, w_dn]
    aliases, carried = {}, 0
    if earlier is not None:
        carried = 2
        aliases = {len(operands) + i: 2 * count + i for i in range(2)}
        in_specs += [pl.BlockSpec(memory_space=pl.ANY)] * 2
        operands += list(earlier)
    out = pl.pallas_call(
        functools.partial(feed_forward_body, count, carried),
        out_shape=[jax.ShapeDtypeStruct((tokens, width), bf16)] * (2 * count)
        + [jax.ShapeDtypeStruct((dy.shape[0], n * hidden), bf16) for n in (1, 2)],
        grid=(hidden // tile,),
        in_specs=in_specs,
        out_specs=[piece] * (2 * count)
        + [pl.BlockSpec((rows, n * tile), lambda j: (block, j)) for n in (1, 2)],
        scratch_shapes=[
            pltpu.VMEM((rows, width), bf16),
            pltpu.VMEM((rows, width), f32),
            pltpu.VMEM((rows, width), f32),
        ],
        input_output_aliases=aliases,
        cost_estimate=pl.CostEstimate(
            flops=12 * rows * width * hidden,
            bytes_accessed=6 * width * hidden + 8 * rows * width + 6 * rows * hidden,
            transcendentals=rows * hidden,
        ),
    )(*operands)
    return out[:count], out[count : 2 * count], out[2 * count :], tile


def fetch(value, k, size):
    return lax.ppermute(value, "fsdp", [((i + k) % size, i) for i in range(size)])


def give(value, k, size):
    return lax.ppermute(value, "fsdp", [(i, (i + k) % size) for i in range(size)])


def gather_pieces(value, size):
    if size != 4:
        return [value] + [fetch(value, k, size) for k in range(1, size)]
    after_one = fetch(value, 1, 4)
    before_one = fetch(value, 3, 4)
    down = lax.ppermute(after_one, "fsdp", [(1, 0), (2, 1)])
    up = lax.ppermute(before_one, "fsdp", [(1, 2), (2, 3)])
    return [value, after_one, jnp.where(lax.axis_index("fsdp") < 2, down, up), before_one]


def scatter_sum(parts, size):
    total = parts[0].astype(f32)
    if size != 4:
        for k in range(1, size):
            total = total + give(parts[k].astype(bf16), k, size).astype(f32)
        return total
    far = parts[2].astype(bf16)
    up = lax.ppermute(far, "fsdp", [(0, 1), (1, 2)])
    down = lax.ppermute(far, "fsdp", [(3, 2), (2, 1)])
    one = (parts[1].astype(f32) + up.astype(f32)).astype(bf16)
    after_one = give(one, 1, 4)
    one = (parts[3].astype(f32) + down.astype(f32)).astype(bf16)
    before_one = give(one, 3, 4)
    return total + after_one.astype(f32) + before_one.astype(f32)


def swap(value, mask):
    size = lax.axis_size("ctx")
    return lax.ppermute(value, "ctx", [(i, i ^ mask) for i in range(size)])


def masks_of(size, first):
    bits = [1 << i for i in range(1, size.bit_length() - 1)]
    return [1] + bits[::-1] if first else bits + [1]


def block_order_of(size):
    found = [0]
    for mask in masks_of(size, False):
        found = found + [m ^ mask for m in found]
    return found


def ctx_gather(value):
    value = value[None]
    for mask in masks_of(lax.axis_size("ctx"), False):
        come = swap(value, mask)
        value = jnp.concatenate([value, come], axis=0)
    return value


def ctx_gather_rows(blocks, share):
    size = lax.axis_size("ctx")
    c = lax.axis_index("ctx")
    fsdp_size, _, width = blocks.shape
    masks = masks_of(size, False)
    value = blocks[None]
    for mask in masks:
        come = swap(value, mask)
        low = (c // mask) % 2 == 0
        value = jnp.stack([jnp.where(low, value, come), jnp.where(low, come, value)])
        value = value.reshape((-1,) + blocks.shape)
    bits = len(masks)
    value = value[:, :, :share].reshape((2,) * bits + (fsdp_size, share, width))
    axes = sorted(range(bits), key=lambda i: -masks[bits - 1 - i])
    value = value.transpose((bits, *axes, bits + 1, bits + 2))
    return value.reshape(-1, width)


def ctx_sum_back(value):
    for mask in masks_of(lax.axis_size("ctx"), True):
        half = value.shape[0] // 2
        come = swap(value[half:], mask)
        value = (value[:half].astype(f32) + come.astype(f32)).astype(value.dtype)
    return value[0]


def ctx_sum_scatter(value):
    size = lax.axis_size("ctx")
    c = lax.axis_index("ctx")

    def halve(v, axis, mask):
        bit = (c // mask) % 2
        kept = lax.dynamic_index_in_dim(v, bit, axis, False)
        sent = lax.dynamic_index_in_dim(v, 1 - bit, axis, False)
        come = swap(sent, mask)
        return (kept.astype(f32) + come.astype(f32)).astype(v.dtype)

    bits = size.bit_length() - 1
    v = value.reshape((2,) * bits + value.shape[1:])
    v = halve(v, bits - 1, 1)
    if bits != 3 or value.shape[1] % 32:
        for axis in range(bits - 2, -1, -1):
            v = halve(v, axis, 1 << (bits - 1 - axis))
        return v
    rows = value.shape[1] // 2
    one, two = halve(v[:, :, :rows], 1, 2), halve(v[:, :, rows:], 0, 4)
    return jnp.concatenate([halve(one, 0, 4), halve(two, 0, 2)], axis=0)


def column_blocks(weight, ctx_size, fsdp_size):
    rows, columns = weight.shape
    share, width = rows // ctx_size, columns // fsdp_size
    part = lax.dynamic_slice_in_dim(weight, lax.axis_index("ctx") * share, share)
    return part.reshape(share, fsdp_size, width).transpose(1, 0, 2)


def swap_blocks(blocks):
    return lax.all_to_all(blocks, "fsdp", split_axis=0, concat_axis=0, tiled=True)


def gather_rows(blocks, share):
    width = blocks.shape[2]
    rows = lax.all_gather(blocks, "ctx", axis=0)[:, :, :share]
    return rows.transpose(1, 0, 2, 3).reshape(-1, width)


def own_rows_of(part, extra):
    F, share, width = part.shape
    C = lax.axis_size("ctx")
    cuts = C // F
    final = width // cuts

    def with_lines(blocks, values):
        if values is None:
            return blocks
        lead, count = values.shape
        rows = -(-count // blocks.shape[2])
        values = jnp.pad(values, ((0, 0), (0, rows * blocks.shape[2] - count)))
        lines = values.reshape(lead, rows, blocks.shape[2]).astype(bf16)
        return jnp.concatenate([blocks, lines], axis=1)

    def total_of(blocks):
        return jnp.sum(blocks[:, share:].astype(f32), axis=0).reshape(-1)[: extra.shape[1]]

    come = swap_blocks(with_lines(part, extra))
    pieces = come[:, :share].reshape(F, share, cuts, final).transpose(0, 2, 1, 3)
    pieces = pieces.reshape(C, share, final)
    lines = None
    if extra is not None:
        lines = jnp.broadcast_to(total_of(come)[None], (C, extra.shape[1]))
    come = lax.all_to_all(with_lines(pieces, lines), "ctx", split_axis=0, concat_axis=0, tiled=True)
    rows = come[:, :share].reshape(C * share, final)
    return rows if extra is None else (rows, total_of(come))


def row_shares(grad, ctx_size, fsdp_size):
    rows, width = grad.shape
    share = rows // (ctx_size * fsdp_size)
    grad = grad.reshape(fsdp_size, ctx_size, share, width).transpose(1, 0, 2, 3)
    return grad.reshape(rows, width)


def joined(parts, axis=0):
    return parts[0] if len(parts) == 1 else jnp.concatenate(parts, axis=axis)


def inverse_norm(values):
    return lax.rsqrt(jnp.mean(values * values, axis=-1, keepdims=True) + rms_eps)


def per_device(
    inputs,
    block_order,
    norm_gains,
    w_query,
    w_key,
    w_value,
    w_output,
    w_gate,
    w_up,
    w_down,
    out_grad,
):
    C = lax.axis_size("ctx")
    F = lax.axis_size("fsdp")
    z = lax.axis_index("fsdp")
    c = lax.axis_index("ctx")
    tokens, width = inputs.shape[1:]
    keys = tokens * C
    own_x, own_dy = inputs[0], out_grad[0]
    sharing = max(1, F // KV_HEADS)
    kv_rows = w_key.shape[0]
    q_rows = w_query.shape[0]
    gain_width = norm_gains.shape[1]
    order = [0, 1, 3, 2] if F == 4 else list(range(F))
    attention_groups = [order]
    backward_groups = [order[:2], order[2:]] if F == 4 else [order]
    ffn_groups = backward_groups if F == 4 else [order[:4], order[4:]]

    x_pieces = gather_pieces(own_x, F)
    w_out_blocks = column_blocks(w_output, C, F)
    share, _ = w_out_blocks.shape[1:]
    gain_blocks = jnp.broadcast_to(norm_gains[None], (F, 2, gain_width))
    swapped = swap_blocks(jnp.concatenate([w_out_blocks, gain_blocks], axis=1))
    w_out = ctx_gather_rows(swapped, share)
    down_blocks = swap_blocks(column_blocks(w_down, C, F))
    gains = swapped[:, share:].transpose(1, 0, 2).reshape(2, F * gain_width)

    half_len = keys // block_order.shape[0]
    offsets = jnp.arange(half_len, dtype=jnp.int32)
    key_pos = (block_order[:, None] * half_len + offsets[None, :]).reshape(keys)
    query_pos = lax.dynamic_slice_in_dim(key_pos, c * tokens, tokens)
    members = jnp.asarray(block_order_of(C), jnp.int32) ^ c
    key_pos = jnp.take(key_pos.reshape(C, tokens), members, axis=0).reshape(keys)
    bias = jnp.where(key_pos[:, None] <= query_pos[None, :], 0.0, masked_score).astype(f32)
    frequency = rope_base ** (-jnp.arange(0, HEAD_DIM, 2).astype(f32) / HEAD_DIM)
    angles = frequency[:, None] * query_pos.astype(f32)[None, :]
    cosine, sine = jnp.cos(angles), jnp.sin(angles)
    gain_one, gain_two = gains[0].astype(f32), gains[1].astype(f32)

    if sharing > 1:
        sharers = [[g * sharing + i for i in range(sharing)] for g in range(F // sharing)]
        both = jnp.stack([w_key, w_value])
        both = lax.all_gather(both, "fsdp", axis=1, tiled=True, axis_index_groups=sharers)
        wk, wv = both[0], both[1]
    else:
        wk, wv = w_key, w_value
    w_qkv = jnp.concatenate([w_query, wk, wv], axis=0)

    def rope(values, sign):
        v = values.reshape(-1, 2, HALF_DIM, values.shape[1] // tokens, tokens)
        cb, sb = cosine[:, None, :], sign * sine[:, None, :]
        top, low = v[:, 0], v[:, 1]
        out = jnp.stack([top * cb - low * sb, low * cb + top * sb], axis=1)
        return out.reshape(values.shape)

    x_float = own_x.astype(f32)
    n1, q, kv, mixed, x_groups, inverses = [], [], [], [], [], []
    attn_parts = [None] * F
    for g, group in enumerate(attention_groups):
        x_group = joined([x_pieces[k] for k in group])
        if g == 0:
            x_group, dy_late = lax.optimization_barrier((x_group, own_dy))
            dy_all = lax.all_gather(dy_late, "fsdp", axis=0)
        inv_group = inverse_norm(x_group.astype(f32))
        n1_group = (x_group.astype(f32) * inv_group * gain_one).astype(bf16)
        x_groups.append(x_group)
        inverses.append(inv_group)
        lin = dot(w_qkv, n1_group, 1, 1)
        q_group = rope(lin[:q_rows], 1.0).astype(bf16) * jnp.asarray(score_scale, bf16)
        kv_own = jnp.concatenate(
            [
                rope(lin[q_rows : q_rows + HEAD_DIM], 1.0).astype(bf16),
                lin[q_rows + HEAD_DIM :].astype(bf16),
            ]
        )
        kv_group = ctx_gather(kv_own)
        q_group, w_out = lax.optimization_barrier((q_group, w_out))
        mixed_group = attend_forward(q_group, kv_group, bias)
        part = dot(mixed_group, w_out, 0, 1)
        for i, k in enumerate(group):
            attn_parts[k] = part[i * tokens : (i + 1) * tokens]
        n1.append(n1_group)
        q.append(q_group)
        kv.append(kv_group)
        mixed.append(mixed_group)
    dy = jnp.concatenate(
        [lax.dynamic_index_in_dim(dy_all, (z + k) % F, 0, False) for k in order], axis=0
    )
    total = scatter_sum(attn_parts, F)
    w_dn = gather_rows(down_blocks, share)
    hidden = x_float + total
    inv_two = inverse_norm(hidden)
    hat_two = hidden * inv_two
    own_n2 = (hat_two * gain_two).astype(bf16)

    n2_pieces = gather_pieces(own_n2, F)
    dn2_parts = [None] * F
    out_parts = [None] * F
    carried, first = None, 0
    for group in ffn_groups:
        pieces = [n2_pieces[k] for k in group]
        dn2_group, out_group, carried, tile = feed_forward(
            pieces, dy, w_gate, w_up, w_dn, first, carried
        )
        for i, k in enumerate(group):
            dn2_parts[k], out_parts[k] = dn2_group[i], out_group[i]
        first += len(group)
    inner, d_both = carried
    n2 = jnp.concatenate([n2_pieces[k] for k in order], axis=0)
    n2, dn2_parts[0] = lax.optimization_barrier((n2, dn2_parts[0]))
    d_n2 = scatter_sum(dn2_parts, F)

    part_down = row_shares(dot(dy, inner, 0, 0).astype(bf16), C, F)
    part_both = dot(d_both, n2, 0, 0).astype(bf16)

    part_down = lax.psum_scatter(part_down, "ctx", scatter_dimension=0, tiled=True)
    grad_both = lax.psum_scatter(part_both, "ctx", scatter_dimension=1, tiled=True)

    scaled = d_n2 * gain_two
    inner_mean = jnp.mean(scaled * hidden, axis=-1, keepdims=True)
    d_hidden = own_dy.astype(f32) + inv_two * scaled - hidden * inv_two**3 * inner_mean
    gain_two_grad = jnp.sum(d_n2 * hat_two, axis=0)
    branch_pieces = gather_pieces(d_hidden.astype(bf16), F)

    *out_parts, branch_pieces[F // 2] = lax.optimization_barrier(
        (*out_parts, branch_pieces[F // 2])
    )
    branch, grads, first = [], None, 0
    for group in backward_groups:
        branch_group = joined([branch_pieces[k] for k in group])
        d_mixed = dot(w_out, branch_group, 0, 1).astype(bf16)
        grads = attend_backward(q[0], kv[0], bias, d_mixed, cosine, sine, first, grads)
        first += len(group)
        branch.append(branch_group)
    d_q, d_kv = [grads[0]], [ctx_sum_back(grads[1])]
    d_qkv = []
    dn1_parts = [None] * F
    gain_one_grad = jnp.zeros((width,), f32)
    for g, group in enumerate(attention_groups):
        dkv_group = d_kv[g].astype(f32)
        if sharing > 1:
            dkv_group = lax.psum(dkv_group, "fsdp", axis_index_groups=sharers)
        d_k = rope(dkv_group[:HEAD_DIM], -1.0).astype(bf16)
        d_v = dkv_group[HEAD_DIM:].astype(bf16)
        if sharing > 1:
            first = (z % sharing) * kv_rows
            d_k = lax.dynamic_slice_in_dim(d_k, first, kv_rows)
            d_v = lax.dynamic_slice_in_dim(d_v, first, kv_rows)
            w_own = jnp.concatenate([w_query, w_key, w_value], axis=0)
        else:
            w_own = w_qkv
        d_qkv.append(jnp.concatenate([d_q[g], d_k, d_v], axis=0))
        part = dot(d_qkv[g], w_own, 0, 0).astype(bf16)
        hat = x_groups[g].astype(f32) * inverses[g]
        gain_one_grad = gain_one_grad + jnp.sum(part.astype(f32) * hat, axis=0)
        for i, k in enumerate(group):
            dn1_parts[k] = part[i * tokens : (i + 1) * tokens]
    d_n1 = scatter_sum(dn1_parts, F)

    layer = hidden + scatter_sum(out_parts, F)
    layer_out = layer.astype(bf16).reshape(1, tokens, width)

    branch, mixed, n1, d_qkv = joined(branch), joined(mixed, 1), joined(n1), joined(d_qkv, 1)
    part_out = row_shares(dot(branch, mixed, 0, 1).astype(bf16), C, F)
    part_out = ctx_sum_scatter(part_out.reshape(C, width // C, -1))
    gain_parts = jnp.stack([gain_one_grad, gain_two_grad]).reshape(2, F, gain_width)
    gain_parts = gain_parts.transpose(1, 0, 2).reshape(F, 2 * gain_width)
    share = width // C // F
    grad_down = own_rows_of(part_down.reshape(F, share, -1), None)
    grad_out, grad_gains = own_rows_of(part_out.reshape(F, share, -1), gain_parts)
    grad_gains = grad_gains.reshape(2, gain_width)
    grad_down, grad_out = grad_down.astype(f32), grad_out.astype(f32)
    g_qkv = dot(n1, d_qkv, 0, 1).astype(bf16)
    g_qkv = ctx_sum_scatter(g_qkv.reshape(C, width // C, -1)).T.astype(f32)
    d_n1, grad_both = lax.optimization_barrier((d_n1, grad_both))
    grad_both = grad_both.reshape(-1, 2, tile, width // C)
    grad_gate = grad_both[:, 0].reshape(-1, width // C).astype(f32)
    grad_up = grad_both[:, 1].reshape(-1, width // C).astype(f32)

    inv_one = inverse_norm(x_float)
    scaled = d_n1 * gain_one
    inner_mean = jnp.mean(scaled * x_float, axis=-1, keepdims=True)
    grad_inputs = d_hidden + inv_one * scaled - x_float * inv_one**3 * inner_mean
    grad_inputs = grad_inputs.reshape(1, tokens, width)
    grad_query = g_qkv[:q_rows]
    grad_key = g_qkv[q_rows : q_rows + kv_rows]
    grad_value = g_qkv[q_rows + kv_rows :]
    return (
        layer_out,
        grad_inputs,
        grad_gains,
        grad_query,
        grad_key,
        grad_value,
        grad_out,
        grad_gate,
        grad_up,
        grad_down,
    )


def solution(mesh):
    rows = P("fsdp", None)
    tokens = P("fsdp", "ctx", None)
    grads = P("fsdp", "ctx")
    return jax.shard_map(
        per_device,
        mesh=mesh,
        in_specs=(tokens, P(), P(None, "fsdp"), rows, rows, rows, rows, rows, rows, rows, tokens),
        out_specs=(tokens, tokens, P(None, "fsdp")) + (grads,) * 7,
        check_vma=False,
    )
```
